32 devices in a mesh: gx: 4 (over z), gy: 8 (over y, x, core).
Axes of the slice: x: 2, y: 2, z: 4, core: 2. Of those that a mesh axis runs over, the one named last changes fastest.
Arguments:
- rock_props: float32 [4, 4, 128, 768], P(None, None, 'gx', 'gy'), may hold values from 0.1 to 10
- block_slot: int32 [128, 768], P('gx', 'gy'), may hold values from 0 to 11, as said below
- bases_start: float32 [12, 4, 256, 1024], P(None, None, 'gx', 'gy'), may hold values from 0.1 to 1
Outputs:
- bases: float32 [12, 4, 256, 1024], P(None, None, 'gx', 'gy')
The draws below stay inside these ranges and needn't reach their ends.
Inputs may be any that keep to these rules, and one draw needn't show every extreme that they name: `block_slot`: within one tile the numbers used are 0 up to some count minus one, each constant on aligned 16 x 16 squares and never falling in row-major order of the squares; the tile at the grid's corner uses all 12.
All inputs are finite; a program needn't handle non-finite values.
Results may differ from the reference program's by a relative error of at most 0.0003.
Values sent between devices are 32-bit elements; how exact they have to be, the bound alone decides.
A program may use at most 64 MiB of HBM per device.

```python
import math
import jax
import jax.numpy as jnp
from jax import lax

TX = 32
TY = 96
NZ = 4
BLK = 16
MARGIN = 16
ITERS = 2
SWEEPS = 3
NB = 12
EX = 64
EY = 128
NX = 128
NY = 768
N_GX = 4
N_GY = 8


def draw_block_slot(key, part):
    sub_x = TX // BLK
    sub_y = TY // BLK
    gx_count = NX // TX
    gy_count = NY // TY
    fresh = jax.random.randint(key, (gx_count, gy_count, sub_x * sub_y), 0, 4) > 0
    first = (jnp.arange(sub_x * sub_y) == 0)[None, None, :]
    corner = (jnp.arange(gx_count)[:, None, None] == 0) & (jnp.arange(gy_count)[None, :, None] == 0)
    starts = (fresh | first | corner).astype(jnp.int32)
    slots = jnp.cumsum(starts, axis=2).astype(jnp.int32) - 1
    slots = slots.reshape(gx_count, gy_count, sub_x, sub_y).transpose(0, 2, 1, 3)
    slots = jnp.repeat(jnp.repeat(slots, BLK, axis=1), BLK, axis=3)
    return slots.reshape(NX, NY).astype(jnp.int32)


def block_levels(own_key, shape, pieces, low, high):
    loudness = 1.0
    for dim, shards_of in pieces:
        draws = jax.random.uniform(jax.random.fold_in(jax.random.fold_in(own_key, 6), dim), (shards_of,), jnp.float32, low / len(pieces), high / len(pieces))
        loudness = loudness * jnp.repeat(jnp.exp(draws), shape[dim] // shards_of).reshape((-1,) + (1,) * (len(shape) - 1 - dim))
    return loudness


def setup_inputs(seed: int = 0) -> dict:
    splits = jax.random.split(jax.random.key(seed), 4)
    rock_props = jnp.clip(jnp.exp(math.log(10.0) - 4.6051702 * jax.random.uniform(splits[0], (4, NZ, NX, NY), jnp.float32) ** block_levels(splits[0], (4, NZ, NX, NY), ((2, 4), (3, 8)), -0.2, 0.2)), 0.1, 10.0)
    block_slot = draw_block_slot(jax.random.fold_in(splits[3], 71), 0)
    bases_start = jnp.clip(0.1 + 0.9 * jax.random.uniform(splits[2], (NB, NZ, N_GX * EX, N_GY * EY), jnp.float32) ** block_levels(splits[2], (NB, NZ, N_GX * EX, N_GY * EY), ((2, 4), (3, 8)), -0.2, 0.2), 0.1, 1.0)
    return {"rock_props": rock_props, "block_slot": block_slot, "bases_start": bases_start}


relax_weight = 2.0 / 3.0


def harmonic(first_k, second_k):
    return 2.0 * first_k * second_k / jnp.maximum(first_k + second_k, 0.1)


def coefficients(perm_x, perm_y, perm_z, storage):
    trans_x = harmonic(perm_x[..., :-1, 1:-1], perm_x[..., 1:, 1:-1])
    trans_y = harmonic(perm_y[..., 1:-1, :-1], perm_y[..., 1:-1, 1:])
    inner_z = perm_z[..., 1:-1, 1:-1]
    trans_z = harmonic(inner_z[..., :-1, :, :], inner_z[..., 1:, :, :])
    zero_layer = jnp.zeros_like(inner_z[..., :1, :, :])
    below = jnp.concatenate([zero_layer, trans_z], axis=-3)
    above = jnp.concatenate([trans_z, zero_layer], axis=-3)
    links = (trans_x[..., :-1, :], trans_x[..., 1:, :], trans_y[..., :-1], trans_y[..., 1:], below, above)
    total = links[0] + links[1] + links[2] + links[3] + links[4] + links[5]
    diagonal = jnp.maximum(total + 0.05 * storage[..., 1:-1, 1:-1], 0.01)
    return links, diagonal


def jacobi_sweep(current, links, diagonal, support):
    width = [(0, 0)] * (current.ndim - 3) + [(1, 1)] * 3
    padded = jnp.pad(current, width)
    neighbour = (links[0] * padded[..., 1:-1, :-2, 1:-1] + links[1] * padded[..., 1:-1, 2:, 1:-1]
                 + links[2] * padded[..., 1:-1, 1:-1, :-2] + links[3] * padded[..., 1:-1, 1:-1, 2:]
                 + links[4] * padded[..., :-2, 1:-1, 1:-1] + links[5] * padded[..., 2:, 1:-1, 1:-1])
    return support * ((1.0 - relax_weight) * current + relax_weight * neighbour / diagonal)


def dilate(own_cells):
    span = 2 * MARGIN + 1
    window_dims = (1,) * (own_cells.ndim - 2) + (span, span)
    return lax.reduce_window(own_cells, jnp.array(0.0, own_cells.dtype), lax.max, window_dims, (1,) * own_cells.ndim, "SAME")


def tile_windows(values, margin):
    leading = values.ndim - 2
    padded = jnp.pad(values, [(0, 0)] * leading + [(margin, margin)] * 2)
    row_windows = jnp.stack([padded[..., tile_no * TX:tile_no * TX + TX + 2 * margin, :] for tile_no in range(N_GX)], 0)
    return jnp.stack([row_windows[..., tile_no * TY:tile_no * TY + TY + 2 * margin] for tile_no in range(N_GY)], 1)


def fold_sum(partial_value):
    layers = partial_value.shape[2]
    summed = jnp.zeros((layers, NX + 2 * MARGIN, NY + 2 * MARGIN), partial_value.dtype)

    def add_window(position, summed):
        row_tile = (position // N_GY).astype(jnp.int32)
        col_tile = (position % N_GY).astype(jnp.int32)
        piece = lax.dynamic_index_in_dim(partial_value, row_tile, 0, keepdims=False)
        piece = lax.dynamic_index_in_dim(piece, col_tile, 0, keepdims=False)
        corner = (jnp.zeros((), jnp.int32), row_tile * TX, col_tile * TY)
        current = lax.dynamic_slice(summed, corner, piece.shape)
        return lax.dynamic_update_slice(summed, current + piece, corner)

    summed = lax.fori_loop(0, N_GX * N_GY, add_window, summed)
    return summed[:, MARGIN:MARGIN + NX, MARGIN:MARGIN + NY]


def reference(rock_props, block_slot, bases_start):
    rock_window = tile_windows(rock_props, MARGIN + 1)
    links, diagonal = coefficients(rock_window[:, :, 0], rock_window[:, :, 1], rock_window[:, :, 2], rock_window[:, :, 3])
    inside = (rock_window[:, :, 0, 0, 1:-1, 1:-1] > 0.0).astype(rock_props.dtype)
    slot_tiles = block_slot.reshape(N_GX, TX, N_GY, TY).transpose(0, 2, 1, 3)
    start_tiles = bases_start.reshape(NB, NZ, N_GX, EX, N_GY, EY).transpose(0, 2, 4, 1, 3, 5)
    slot_ids = jnp.arange(NB, dtype=jnp.int32)
    margin = MARGIN

    def own_of(slot):
        own_cells = (slot_tiles == slot).astype(rock_props.dtype)
        return jnp.pad(own_cells, ((0, 0), (0, 0), (margin, margin), (margin, margin)))

    def region_of(slot):
        return (dilate(own_of(slot)) * inside)[:, :, None]

    def initial(pair):
        start, slot = pair
        return region_of(slot) * (own_of(slot)[:, :, None] + start)

    bases_now = lax.map(initial, (start_tiles, slot_ids))
    for turn in range(ITERS):
        def relax_slot(pair):
            current, slot = pair
            region = region_of(slot)
            for sweep_no in range(SWEEPS):
                current = jacobi_sweep(current, links, diagonal, region)
            return current

        bases_now = lax.map(relax_slot, (bases_now, slot_ids))
        partial_value = jnp.sum(bases_now, axis=0)
        sums = tile_windows(fold_sum(partial_value), MARGIN)
        bases_now = bases_now / jnp.maximum(sums, 0.01)
    return bases_now.transpose(0, 3, 1, 4, 2, 5).reshape(NB, NZ, N_GX * EX, N_GY * EY)
```

```python
import functools

import jax
import jax.numpy as jnp
from jax import lax
from jax.experimental import pallas as pl
from jax.experimental.pallas import tpu as pltpu
from jax.sharding import PartitionSpec as P

MARGIN = 16
BLK = 16
ITERS = 2
SWEEPS = 3
PAD = 8
LANES = 128
COLOURS = 3
WEIGHT = 2.0 / 3.0
MESH = pl.DeviceIdType.MESH
DIRS = ((-1, -1), (1, -1), (-1, 1), (1, 1), (0, -1), (0, 1), (-1, 0), (1, 0))


def harmonic(first_k, second_k):
    return 2.0 * first_k * second_k / jnp.maximum(first_k + second_k, 0.1)


def tall(value, count):
    return jnp.concatenate([value] * count, axis=0)


def kernel(
    n_gx, n_gy,
    rock_hbm, slot_ref, start_hbm, out_hbm,
    rock, start, window, joined, strip_out, strip_in, coef, maps, span_map, packed, spanning,
    part, part_strip, part_x, part_y, part_d,
    rock_sem, start_sem, out_sem, send_sem, recv_sem,
):
    m = MARGIN
    nb, nz, ex, ey = start.shape
    tx, ty = rock.shape[2], rock.shape[3]
    rows_p = BLK + 2 * m
    full = ex + 2 * PAD
    n_win = window.shape[0]
    KX, KY, ST, TZ = 0, nz, 2 * nz, 3 * nz
    sub_y = ty // BLK
    half = ex // 2

    gx = lax.axis_index("gx")
    gy = lax.axis_index("gy")

    def exists(dx, dy):
        ok = None
        for cond in (
            [gx > 0] if dx < 0 else [gx < n_gx - 1] if dx > 0 else []
        ) + ([gy > 0] if dy < 0 else [gy < n_gy - 1] if dy > 0 else []):
            ok = cond if ok is None else jnp.logical_and(ok, cond)
        return ok

    rock_copy = pltpu.make_async_copy(rock_hbm, rock, rock_sem)
    start_copy = pltpu.make_async_copy(start_hbm, start, start_sem)
    rock_copy.start()
    start_copy.start()

    for i in range(n_win):
        window[i, : PAD + m, :] = jnp.zeros((PAD + m, ey), jnp.float32)
        window[i, PAD + m + tx :, :] = jnp.zeros((PAD + m, ey), jnp.float32)
    strip_in[...] = jnp.zeros_like(strip_in)
    part_x[...] = jnp.zeros_like(part_x)
    part_y[...] = jnp.zeros_like(part_y)
    part_d[...] = jnp.zeros_like(part_d)

    barrier = pltpu.get_barrier_semaphore()
    expected = jnp.int32(0)
    for dx, dy in DIRS:
        there = exists(dx, dy)
        expected = expected + there.astype(jnp.int32)

        @pl.when(there)
        def _(dx=dx, dy=dy):
            pl.semaphore_signal(
                barrier, inc=1, device_id=(gx + dx, gy + dy), device_id_type=MESH
            )

    def rock_messages(dx, dy):
        if dy == 0:
            if dx < 0:
                return [
                    (window.at[0:nz, pl.ds(PAD + m, m + PAD)], window.at[0:nz, pl.ds(PAD + m + tx, m + PAD)]),
                    (window.at[nz:n_win, pl.ds(PAD + m, m)], window.at[nz:n_win, pl.ds(PAD + m + tx, m)]),
                ]
            return [
                (window.at[0:nz, pl.ds(tx, m + PAD)], window.at[0:nz, pl.ds(0, m + PAD)]),
                (window.at[nz:n_win, pl.ds(PAD + tx, m)], window.at[nz:n_win, pl.ds(PAD, m)]),
            ]
        side = 0 if dy < 0 else 1
        if dx == 0:
            return [(strip_out.at[side], strip_in.at[side, :, pl.ds(PAD + m, tx)])]
        if dx < 0:
            return [(strip_out.at[side, :, pl.ds(0, m + PAD)], strip_in.at[side, :, pl.ds(PAD + m + tx, m + PAD)])]
        return [(strip_out.at[side, :, pl.ds(tx - m - PAD, m + PAD)], strip_in.at[side, :, pl.ds(0, m + PAD)])]

    def sum_messages(turn, dx, dy):
        if dy == 0:
            if dx < 0:
                return [(part.at[turn, :, pl.ds(0, half)], part_x.at[turn, :, pl.ds(half, half)])]
            return [(part.at[turn, :, pl.ds(half, half)], part_x.at[turn, :, pl.ds(0, half)])]
        side = 0 if dy < 0 else 1
        if dx == 0:
            return [(part_strip.at[turn, side], part_y.at[turn, side])]
        if dx < 0:
            return [(part_strip.at[turn, side, pl.ds(0, half)], part_d.at[turn, side, pl.ds(half, half)])]
        return [(part_strip.at[turn, side, pl.ds(half, half)], part_d.at[turn, side, pl.ds(0, half)])]

    def copies(phase, dx, dy):
        messages = rock_messages(dx, dy) if phase == 0 else sum_messages(phase - 1, dx, dy)
        base = 2 * DIRS.index((dx, dy))
        return [
            pltpu.make_async_remote_copy(
                src_ref=src,
                dst_ref=dst,
                send_sem=send_sem.at[phase, base + i],
                recv_sem=recv_sem.at[phase, base + i],
                device_id=(gx + dx, gy + dy),
                device_id_type=MESH,
            )
            for i, (src, dst) in enumerate(messages)
        ]

    def send(phase):
        for dx, dy in DIRS:
            @pl.when(exists(dx, dy))
            def _(dx=dx, dy=dy):
                for copy in copies(phase, dx, dy):
                    copy.start()

    def receive(phase):
        for dx, dy in DIRS:
            @pl.when(exists(-dx, -dy))
            def _(dx=dx, dy=dy):
                for copy in copies(phase, dx, dy):
                    copy.wait_recv()

    def sent(phase):
        for dx, dy in DIRS:
            @pl.when(exists(dx, dy))
            def _(dx=dx, dy=dy):
                for copy in copies(phase, dx, dy):
                    copy.wait_send()

    rock_copy.wait()
    lane_t = lax.broadcasted_iota(jnp.int32, (tx, ey), 1)
    own_rows = slice(PAD + m, PAD + m + tx)

    def place(i, value):
        wide = jnp.concatenate([value, jnp.zeros((tx, ey - ty), jnp.float32)], axis=1)
        window[i, own_rows, :] = pltpu.roll(wide, m, axis=1)

    for z in range(nz):
        place(KX + z, rock[0, z])
        place(KY + z, rock[1, z])
        place(ST + z, rock[3, z])
        if z < nz - 1:
            place(TZ + z, harmonic(rock[2, z], rock[2, z + 1]))
    per = LANES // m
    for side in range(2):
        first = m if side == 0 else m + ty - m
        extra = 2 * m if side == 0 else m + ty - m - 1
        for block in range(2):
            packed_strip = jnp.zeros((tx, ey), jnp.float32)
            for i in range(block * per, min(n_win, block * per + per)):
                j = i - block * per
                moved = pltpu.roll(window[i, own_rows, :], (m * j - first) % ey, axis=1)
                packed_strip = jnp.where(lane_t // m == j, moved, packed_strip)
            if block == 1:
                for z in range(nz):
                    spot = m * (per - 1) + z
                    moved = pltpu.roll(window[KY + z, own_rows, :], (spot - extra) % ey, axis=1)
                    packed_strip = jnp.where(lane_t == spot, moved, packed_strip)
            strip_out[side, block] = packed_strip

    pl.semaphore_wait(barrier, expected)
    send(0)

    lane = lax.broadcasted_iota(jnp.int32, (PAD, ey), 1)
    slot_rows = []
    for r in range(2):
        raw = slot_ref[r * BLK : r * BLK + PAD, :].astype(jnp.float32)
        wide = jnp.concatenate([raw, jnp.full((PAD, ey - ty), -9.0, jnp.float32)], axis=1)
        slot_rows.append(pltpu.roll(wide, m, axis=1))
    in_tile = jnp.logical_and(lane >= m, lane < m + ty)
    last = jnp.max(slot_rows[0], axis=1, keepdims=True)
    first = jnp.min(jnp.where(in_tile, slot_rows[1], 99.0), axis=1, keepdims=True)
    span = jnp.broadcast_to(jnp.where(last == first, last, -5.0), (PAD, ey))
    reach = []
    for r in range(2):
        near = (slot_rows[r], pltpu.roll(slot_rows[r], m, axis=1), pltpu.roll(slot_rows[r], ey - m, axis=1))
        touched = jnp.zeros((PAD, ey), jnp.float32)
        for value in near:
            touched = jnp.where(value == span, 1.0, touched)
        reach.append(touched)
        for c in range(COLOURS):
            held = jnp.full((PAD, ey), -1.0, jnp.float32)
            for value in near:
                colour = value - COLOURS * jnp.floor((value + 0.5) / COLOURS)
                fits = jnp.logical_and(value >= 0.0, jnp.logical_and(colour == float(c), value != span))
                held = jnp.where(fits, value, held)
            a = r * COLOURS + c
            maps[a, 0] = held
            taken = held >= 0.0
            low = jnp.logical_and(taken, jnp.logical_and(lane > 0, pltpu.roll(held, 1, axis=1) == held))
            high = jnp.logical_and(taken, jnp.logical_and(lane < ey - 1, pltpu.roll(held, ey - 1, axis=1) == held))
            maps[a, 1] = jnp.where(low, 1.0, 0.0)
            maps[a, 2] = jnp.where(high, 1.0, 0.0)
    both = jnp.maximum(reach[0], reach[1])
    span_map[...] = jnp.concatenate(
        [tall(reach[0], BLK // PAD), tall(both, (ex - 2 * BLK) // PAD), tall(reach[1], BLK // PAD)], axis=0
    )

    row = lax.broadcasted_iota(jnp.int32, (ex, ey), 0)
    col = lax.broadcasted_iota(jnp.int32, (ex, ey), 1)
    inside = jnp.ones((ex, ey), jnp.float32)
    edge = lambda cond: jnp.where(cond, 0.0, 1.0).astype(jnp.float32)
    inside = inside * jnp.where(row < m, edge(gx == 0), 1.0)
    inside = inside * jnp.where(row >= m + tx, edge(gx == n_gx - 1), 1.0)
    inside = inside * jnp.where(col < m, edge(gy == 0), 1.0)
    inside = inside * jnp.where(col >= m + ty, edge(gy == n_gy - 1), 1.0)

    packed[:, :, :, :PAD, :] = jnp.zeros(packed.shape[:3] + (PAD, ey), jnp.float32)
    packed[:, :, :, PAD + rows_p :, :] = jnp.zeros(packed.shape[:3] + (PAD, ey), jnp.float32)
    spanning[:, :, :PAD, :] = jnp.zeros(spanning.shape[:2] + (PAD, ey), jnp.float32)
    spanning[:, :, PAD + ex :, :] = jnp.zeros(spanning.shape[:2] + (PAD, ey), jnp.float32)
    mid = slice(PAD, PAD + rows_p)
    mid_s = slice(PAD, PAD + ex)
    n_p = rows_p // PAD
    n_s = ex // PAD
    start_copy.wait()

    def fill(z, carry):
        for r in range(2):
            rows = slice(r * BLK, r * BLK + rows_p)
            slot_count = sub_y if r == 0 else nb
            for c in range(COLOURS):
                a = r * COLOURS + c
                held = maps[a, 0]
                own = jnp.where(held == slot_rows[r], 1.0, 0.0)
                none = jnp.zeros((m, ey), jnp.float32)
                value = jnp.concatenate([none, tall(own, BLK // PAD), none], axis=0)
                held_tall = tall(held, n_p)
                for k in range(c, slot_count, COLOURS):
                    value = value + jnp.where(held_tall == float(k), start[k, z, rows, :], 0.0)
                packed[0, a, z, mid, :] = value * inside[rows]
        none = jnp.zeros((m, ey), jnp.float32)
        value = jnp.concatenate(
            [none]
            + [tall(jnp.where(slot_rows[r] == span, 1.0, 0.0), BLK // PAD) for r in range(2)]
            + [none],
            axis=0,
        )
        span_tall = tall(span, n_s)
        for k in range(sub_y):
            value = value + jnp.where(span_tall == float(k), start[k, z], 0.0)
        spanning[0, z, mid_s, :] = value * inside * span_map[...]
        return carry

    lax.fori_loop(0, nz, fill, 0)

    receive(0)
    lane_f = lax.broadcasted_iota(jnp.int32, (full, ey), 1)
    for i in range(n_win):
        block, j = i // per, i % per
        left = pltpu.roll(strip_in[1, block], (-m * j) % ey, axis=1)
        right = pltpu.roll(strip_in[0, block], (ey - m - m * j) % ey, axis=1)
        joined[i] = jnp.where(lane_f < m, left, jnp.where(lane_f >= ey - m, right, window[i]))
    lane_s = lax.broadcasted_iota(jnp.int32, (ex, ey), 1)
    for z in range(nz):
        here = joined[KX + z, mid_s, :]
        link_xl = harmonic(joined[KX + z, PAD - 1 : PAD - 1 + ex, :], here)
        link_xh = harmonic(here, joined[KX + z, PAD + 1 : PAD + 1 + ex, :])
        here = joined[KY + z, mid_s, :]
        spot = m * (per - 1) + z
        outer = pltpu.roll(strip_in[1, 1, mid_s, :], (-spot) % ey, axis=1)
        link_yl = harmonic(jnp.where(lane_s == 0, outer, pltpu.roll(here, 1, axis=1)), here)
        outer = pltpu.roll(strip_in[0, 1, mid_s, :], (ey - 1 - spot) % ey, axis=1)
        link_yh = harmonic(here, jnp.where(lane_s == ey - 1, outer, pltpu.roll(here, ey - 1, axis=1)))
        links = [link_xl, link_xh, link_yl, link_yh]
        places = [0, 1, 2, 3]
        if z > 0:
            links.append(joined[TZ + z - 1, mid_s, :])
            places.append(4)
        if z < nz - 1:
            links.append(joined[TZ + z, mid_s, :])
            places.append(5)
        total = links[0]
        for link in links[1:]:
            total = total + link
        diagonal = jnp.maximum(total + 0.05 * joined[ST + z, mid_s, :], 0.01)
        factor = WEIGHT / diagonal
        for place_no, link in zip(places, links):
            coef[place_no, z] = link * factor

    stay = 1.0 - WEIGHT

    def sweep(s, carry):
        src = lax.rem(s, 2)
        dst = 1 - src

        def colour_step(c, carry2):
            for r in range(2):
                a = r * COLOURS + c
                rows = slice(r * BLK, r * BLK + rows_p)
                low = tall(maps[a, 1], n_p)
                high = tall(maps[a, 2], n_p)
                for z in range(nz):
                    cur = packed[src, a, z, mid, :]
                    new = stay * cur
                    new = new + coef[0, z, rows, :] * packed[src, a, z, PAD - 1 : PAD - 1 + rows_p, :]
                    new = new + coef[1, z, rows, :] * packed[src, a, z, PAD + 1 : PAD + 1 + rows_p, :]
                    new = new + coef[2, z, rows, :] * (pltpu.roll(cur, 1, axis=1) * low)
                    new = new + coef[3, z, rows, :] * (pltpu.roll(cur, ey - 1, axis=1) * high)
                    if z > 0:
                        new = new + coef[4, z, rows, :] * packed[src, a, z - 1, mid, :]
                    if z < nz - 1:
                        new = new + coef[5, z, rows, :] * packed[src, a, z + 1, mid, :]
                    packed[dst, a, z, mid, :] = new
            return carry2

        lax.fori_loop(0, COLOURS, colour_step, 0)
        for z in range(nz):
            cur = spanning[src, z, mid_s, :]
            new = stay * cur
            new = new + coef[0, z] * spanning[src, z, PAD - 1 : PAD - 1 + ex, :]
            new = new + coef[1, z] * spanning[src, z, PAD + 1 : PAD + 1 + ex, :]
            new = new + coef[2, z] * jnp.where(lane_s > 0, pltpu.roll(cur, 1, axis=1), 0.0)
            new = new + coef[3, z] * jnp.where(lane_s < ey - 1, pltpu.roll(cur, ey - 1, axis=1), 0.0)
            if z > 0:
                new = new + coef[4, z] * spanning[src, z - 1, mid_s, :]
            if z < nz - 1:
                new = new + coef[5, z] * spanning[src, z + 1, mid_s, :]
            spanning[dst, z, mid_s, :] = new * span_map[...]
        return carry

    width = 2 * m
    for turn in range(ITERS):
        lax.fori_loop(0, SWEEPS, sweep, 0)
        end = SWEEPS % 2
        strips = [jnp.zeros((ex, ey), jnp.float32) for _ in range(2)]
        for z in range(nz):
            sums = []
            for r in range(2):
                value = packed[end, r * COLOURS, z, mid, :]
                for c in range(1, COLOURS):
                    value = value + packed[end, r * COLOURS + c, z, mid, :]
                sums.append(value)
            gap = jnp.zeros((ex - rows_p, ey), jnp.float32)
            value = (
                spanning[end, z, mid_s, :]
                + jnp.concatenate([sums[0], gap], axis=0)
                + jnp.concatenate([gap, sums[1]], axis=0)
            )
            part[turn, z] = value
            for side in range(2):
                first_lane = 0 if side == 0 else ey - width
                moved = pltpu.roll(value, (width * z - first_lane) % ey, axis=1)
                strips[side] = jnp.where(lane_s // width == z, moved, strips[side])
        for side in range(2):
            part_strip[turn, side] = strips[side]
        send(turn + 1)
        receive(turn + 1)
        from_right = part_y[turn, 0] + part_d[turn, 0]
        from_left = part_y[turn, 1] + part_d[turn, 1]
        final = turn == ITERS - 1
        for z in range(nz):
            left = pltpu.roll(from_left, (-width * z) % ey, axis=1)
            right = pltpu.roll(from_right, (ey - width - width * z) % ey, axis=1)
            total = part[turn, z] + part_x[turn, z]
            total = total + jnp.where(lane_s < width, left, jnp.where(lane_s >= ey - width, right, 0.0))
            scale = 1.0 / jnp.maximum(total, 0.01)
            for r in range(2):
                rows = slice(r * BLK, r * BLK + rows_p)
                for c in range(COLOURS):
                    a = r * COLOURS + c
                    packed[0, a, z, mid, :] = packed[end, a, z, mid, :] * scale[rows]
            spanning[0, z, mid_s, :] = spanning[end, z, mid_s, :] * scale

    def unpack(z, carry):
        span_tall = tall(span, n_s)
        whole = spanning[0, z, mid_s, :]
        gap = jnp.zeros((ex - rows_p, ey), jnp.float32)
        for k in range(nb):
            c = k % COLOURS
            a = COLOURS + c
            value = jnp.where(tall(maps[a, 0], n_p) == float(k), packed[0, a, z, mid, :], 0.0)
            value = jnp.concatenate([gap, value], axis=0)
            if k < sub_y:
                top = jnp.where(tall(maps[c, 0], n_p) == float(k), packed[0, c, z, mid, :], 0.0)
                value = value + jnp.concatenate([top, gap], axis=0)
                value = value + jnp.where(span_tall == float(k), whole, 0.0)
            start[k, z] = value
        pltpu.make_async_copy(start.at[:, z], out_hbm.at[:, z], out_sem.at[z]).start()
        return carry

    lax.fori_loop(0, nz, unpack, 0)
    for z in range(nz):
        pltpu.make_async_copy(start.at[:, z], out_hbm.at[:, z], out_sem.at[z]).wait()
    for phase in range(ITERS + 1):
        sent(phase)


def solution(mesh):
    n_gx, n_gy = mesh.shape["gx"], mesh.shape["gy"]

    def body(rock_props, block_slot, bases_start):
        nb, nz, ex, ey = bases_start.shape
        n_win = 4 * nz - 1
        full = ex + 2 * PAD
        rows_p = BLK + 2 * MARGIN + 2 * PAD
        f32 = jnp.float32
        tx = block_slot.shape[0]
        return pl.pallas_call(
            functools.partial(kernel, n_gx, n_gy),
            out_shape=jax.ShapeDtypeStruct(bases_start.shape, f32),
            in_specs=[
                pl.BlockSpec(memory_space=pl.ANY),
                pl.BlockSpec(memory_space=pltpu.VMEM),
                pl.BlockSpec(memory_space=pl.ANY),
            ],
            out_specs=pl.BlockSpec(memory_space=pl.ANY),
            scratch_shapes=[
                pltpu.VMEM(rock_props.shape, f32),
                pltpu.VMEM(bases_start.shape, f32),
                pltpu.VMEM((n_win, full, ey), f32),
                pltpu.VMEM((n_win, full, ey), f32),
                pltpu.VMEM((2, 2, tx, ey), f32),
                pltpu.VMEM((2, 2, full, ey), f32),
                pltpu.VMEM((6, nz, ex, ey), f32),
                pltpu.VMEM((2 * COLOURS, 3, PAD, ey), f32),
                pltpu.VMEM((ex, ey), f32),
                pltpu.VMEM((2, 2 * COLOURS, nz, rows_p, ey), f32),
                pltpu.VMEM((2, nz, full, ey), f32),
                pltpu.VMEM((ITERS, nz, ex, ey), f32),
                pltpu.VMEM((ITERS, 2, ex, ey), f32),
                pltpu.VMEM((ITERS, nz, ex, ey), f32),
                pltpu.VMEM((ITERS, 2, ex, ey), f32),
                pltpu.VMEM((ITERS, 2, ex, ey), f32),
                pltpu.SemaphoreType.DMA,
                pltpu.SemaphoreType.DMA,
                pltpu.SemaphoreType.DMA((nz,)),
                pltpu.SemaphoreType.DMA((ITERS + 1, 2 * len(DIRS))),
                pltpu.SemaphoreType.DMA((ITERS + 1, 2 * len(DIRS))),
            ],
            compiler_params=pltpu.CompilerParams(collective_id=0, has_side_effects=True),
        )(rock_props, block_slot, bases_start)

    placed = (P(None, None, "gx", "gy"), P("gx", "gy"), P(None, None, "gx", "gy"))
    return jax.shard_map(
        body, mesh=mesh, in_specs=placed, out_specs=P(None, None, "gx", "gy"), check_vma=False
    )
```

```python
import functools

import jax
import jax.numpy as jnp
from jax import lax
from jax.experimental import pallas as pl
from jax.experimental.pallas import tpu as pltpu
from jax.sharding import PartitionSpec as P

MARGIN = 16
BLK = 16
ITERS = 2
SWEEPS = 3
PAD = 8
LANES = 128
COLOURS = 3
WEIGHT = 2.0 / 3.0
MESH = pl.DeviceIdType.MESH
DIRS = ((-1, -1), (1, -1), (-1, 1), (1, 1), (0, -1), (0, 1), (-1, 0), (1, 0))


def harmonic(first_k, second_k):
    return 2.0 * first_k * second_k / jnp.maximum(first_k + second_k, 0.1)


def tall(value, count):
    return jnp.concatenate([value] * count, axis=0)


def kernel(
    n_gx, n_gy,
    rock_hbm, slot_ref, start_hbm, packed_a, spanning_a, held_out, span_out,
    rock, start, window, joined, strip_out, strip_in, coef, coef_y, same, span_map, packed_b, spanning_b,
    part, part_strip, part_x, part_y, part_d,
    rock_sem, start_sem, send_sem, recv_sem,
):
    m = MARGIN
    nb, nz, ex, ey = start.shape
    tx, ty = rock.shape[2], rock.shape[3]
    rows_p = BLK + 2 * m
    full = ex + 2 * PAD
    n_win = window.shape[0]
    KX, KY, ST, TZ = 0, nz, 2 * nz, 3 * nz
    sub_y = ty // BLK
    half = ex // 2

    gx = lax.axis_index("gx")
    gy = lax.axis_index("gy")

    def exists(dx, dy):
        ok = None
        for cond in (
            [gx > 0] if dx < 0 else [gx < n_gx - 1] if dx > 0 else []
        ) + ([gy > 0] if dy < 0 else [gy < n_gy - 1] if dy > 0 else []):
            ok = cond if ok is None else jnp.logical_and(ok, cond)
        return ok

    rock_copy = pltpu.make_async_copy(rock_hbm, rock, rock_sem)
    start_copy = pltpu.make_async_copy(start_hbm, start, start_sem)
    rock_copy.start()
    start_copy.start()

    for i in range(n_win):
        window[i, : PAD + m, :] = jnp.zeros((PAD + m, ey), jnp.float32)
        window[i, PAD + m + tx :, :] = jnp.zeros((PAD + m, ey), jnp.float32)
    strip_in[...] = jnp.zeros_like(strip_in)
    part_x[...] = jnp.zeros_like(part_x)
    part_y[...] = jnp.zeros_like(part_y)
    part_d[...] = jnp.zeros_like(part_d)

    barrier = pltpu.get_barrier_semaphore()
    expected = jnp.int32(0)
    for dx, dy in DIRS:
        there = exists(dx, dy)
        expected = expected + there.astype(jnp.int32)

        @pl.when(there)
        def _(dx=dx, dy=dy):
            pl.semaphore_signal(
                barrier, inc=1, device_id=(gx + dx, gy + dy), device_id_type=MESH
            )

    def rock_messages(dx, dy):
        if dy == 0:
            if dx < 0:
                return [
                    (window.at[0:nz, pl.ds(PAD + m, m + PAD)], window.at[0:nz, pl.ds(PAD + m + tx, m + PAD)]),
                    (window.at[nz:n_win, pl.ds(PAD + m, m)], window.at[nz:n_win, pl.ds(PAD + m + tx, m)]),
                ]
            return [
                (window.at[0:nz, pl.ds(tx, m + PAD)], window.at[0:nz, pl.ds(0, m + PAD)]),
                (window.at[nz:n_win, pl.ds(PAD + tx, m)], window.at[nz:n_win, pl.ds(PAD, m)]),
            ]
        side = 0 if dy < 0 else 1
        if dx == 0:
            return [(strip_out.at[side], strip_in.at[side, :, pl.ds(PAD + m, tx)])]
        if dx < 0:
            return [(strip_out.at[side, :, pl.ds(0, m + PAD)], strip_in.at[side, :, pl.ds(PAD + m + tx, m + PAD)])]
        return [(strip_out.at[side, :, pl.ds(tx - m - PAD, m + PAD)], strip_in.at[side, :, pl.ds(0, m + PAD)])]

    def sum_messages(turn, dx, dy):
        if dy == 0:
            if dx < 0:
                return [(part.at[turn, :, pl.ds(0, half)], part_x.at[turn, :, pl.ds(half, half)])]
            return [(part.at[turn, :, pl.ds(half, half)], part_x.at[turn, :, pl.ds(0, half)])]
        side = 0 if dy < 0 else 1
        if dx == 0:
            return [(part_strip.at[turn, side], part_y.at[turn, side])]
        if dx < 0:
            return [(part_strip.at[turn, side, pl.ds(0, half)], part_d.at[turn, side, pl.ds(half, half)])]
        return [(part_strip.at[turn, side, pl.ds(half, half)], part_d.at[turn, side, pl.ds(0, half)])]

    def copies(phase, dx, dy):
        messages = rock_messages(dx, dy) if phase == 0 else sum_messages(phase - 1, dx, dy)
        base = 2 * DIRS.index((dx, dy))
        return [
            pltpu.make_async_remote_copy(
                src_ref=src,
                dst_ref=dst,
                send_sem=send_sem.at[phase, base + i],
                recv_sem=recv_sem.at[phase, base + i],
                device_id=(gx + dx, gy + dy),
                device_id_type=MESH,
            )
            for i, (src, dst) in enumerate(messages)
        ]

    def send(phase):
        for dx, dy in DIRS:
            @pl.when(exists(dx, dy))
            def _(dx=dx, dy=dy):
                for copy in copies(phase, dx, dy):
                    copy.start()

    def receive(phase):
        for dx, dy in DIRS:
            @pl.when(exists(-dx, -dy))
            def _(dx=dx, dy=dy):
                for copy in copies(phase, dx, dy):
                    copy.wait_recv()

    def sent(phase):
        for dx, dy in DIRS:
            @pl.when(exists(dx, dy))
            def _(dx=dx, dy=dy):
                for copy in copies(phase, dx, dy):
                    copy.wait_send()

    rock_copy.wait()
    lane_t = lax.broadcasted_iota(jnp.int32, (tx, ey), 1)
    own_rows = slice(PAD + m, PAD + m + tx)

    def place(i, value):
        wide = jnp.concatenate([value, jnp.zeros((tx, ey - ty), jnp.float32)], axis=1)
        window[i, own_rows, :] = pltpu.roll(wide, m, axis=1)

    for z in range(nz):
        place(KX + z, rock[0, z])
        place(KY + z, rock[1, z])
        place(ST + z, rock[3, z])
        if z < nz - 1:
            place(TZ + z, harmonic(rock[2, z], rock[2, z + 1]))
    per = LANES // m
    for side in range(2):
        first = m if side == 0 else m + ty - m
        extra = 2 * m if side == 0 else m + ty - m - 1
        for block in range(2):
            packed_strip = jnp.zeros((tx, ey), jnp.float32)
            for i in range(block * per, min(n_win, block * per + per)):
                j = (i - block * per - (1 - side)) % per
                moved = pltpu.roll(window[i, own_rows, :], (m * j - first) % ey, axis=1)
                packed_strip = jnp.where(lane_t // m == j, moved, packed_strip)
            if block == 1:
                for z in range(nz):
                    spot = m * (per - 2 + side) + z
                    moved = pltpu.roll(window[KY + z, own_rows, :], (spot - extra) % ey, axis=1)
                    packed_strip = jnp.where(lane_t == spot, moved, packed_strip)
            strip_out[side, block] = packed_strip

    pl.semaphore_wait(barrier, expected)
    send(0)

    lane = lax.broadcasted_iota(jnp.int32, (PAD, ey), 1)
    slot_rows = []
    for r in range(2):
        raw = slot_ref[r * BLK : r * BLK + PAD, :].astype(jnp.float32)
        wide = jnp.concatenate([raw, jnp.full((PAD, ey - ty), -9.0, jnp.float32)], axis=1)
        slot_rows.append(pltpu.roll(wide, m, axis=1))
    in_tile = jnp.logical_and(lane >= m, lane < m + ty)
    last = jnp.max(slot_rows[0], axis=1, keepdims=True)
    first = jnp.min(jnp.where(in_tile, slot_rows[1], 99.0), axis=1, keepdims=True)
    span = jnp.broadcast_to(jnp.where(last == first, last, -5.0), (PAD, ey))
    reach = []
    for r in range(2):
        near = (slot_rows[r], pltpu.roll(slot_rows[r], m, axis=1), pltpu.roll(slot_rows[r], ey - m, axis=1))
        touched = jnp.zeros((PAD, ey), jnp.float32)
        for value in near:
            touched = jnp.where(value == span, 1.0, touched)
        reach.append(touched)
        for c in range(COLOURS):
            held = jnp.full((PAD, ey), -1.0, jnp.float32)
            for value in near:
                colour = value - COLOURS * jnp.floor((value + 0.5) / COLOURS)
                fits = jnp.logical_and(value >= 0.0, jnp.logical_and(colour == float(c), value != span))
                held = jnp.where(fits, value, held)
            a = r * COLOURS + c
            held_out[a] = held
            taken = held >= 0.0
            low = jnp.logical_and(taken, jnp.logical_and(lane > 0, pltpu.roll(held, 1, axis=1) == held))
            high = jnp.logical_and(taken, jnp.logical_and(lane < ey - 1, pltpu.roll(held, ey - 1, axis=1) == held))
            same[a, 0] = jnp.where(low, 1.0, 0.0)
            same[a, 1] = jnp.where(high, 1.0, 0.0)
    span_out[...] = span
    both = jnp.maximum(reach[0], reach[1])
    span_map[...] = jnp.concatenate(
        [tall(reach[0], BLK // PAD), tall(both, (ex - 2 * BLK) // PAD), tall(reach[1], BLK // PAD)], axis=0
    )

    row = lax.broadcasted_iota(jnp.int32, (ex, ey), 0)
    col = lax.broadcasted_iota(jnp.int32, (ex, ey), 1)
    inside = jnp.ones((ex, ey), jnp.float32)
    edge = lambda cond: jnp.where(cond, 0.0, 1.0).astype(jnp.float32)
    inside = inside * jnp.where(row < m, edge(gx == 0), 1.0)
    inside = inside * jnp.where(row >= m + tx, edge(gx == n_gx - 1), 1.0)
    inside = inside * jnp.where(col < m, edge(gy == 0), 1.0)
    inside = inside * jnp.where(col >= m + ty, edge(gy == n_gy - 1), 1.0)

    for ref in (packed_a, packed_b):
        ref[:, :, :PAD, :] = jnp.zeros(ref.shape[:2] + (PAD, ey), jnp.float32)
        ref[:, :, PAD + rows_p :, :] = jnp.zeros(ref.shape[:2] + (PAD, ey), jnp.float32)
    for ref in (spanning_a, spanning_b):
        ref[:, :PAD, :] = jnp.zeros((nz, PAD, ey), jnp.float32)
        ref[:, PAD + ex :, :] = jnp.zeros((nz, PAD, ey), jnp.float32)
    mid = slice(PAD, PAD + rows_p)
    mid_s = slice(PAD, PAD + ex)
    n_p = rows_p // PAD
    n_s = ex // PAD
    start_copy.wait()

    def fill(z, carry):
        for r in range(2):
            rows = slice(r * BLK, r * BLK + rows_p)
            slot_count = sub_y if r == 0 else nb
            for c in range(COLOURS):
                a = r * COLOURS + c
                held = held_out[a]
                own = jnp.where(held == slot_rows[r], 1.0, 0.0)
                none = jnp.zeros((m, ey), jnp.float32)
                value = jnp.concatenate([none, tall(own, BLK // PAD), none], axis=0)
                held_tall = tall(held, n_p)
                for k in range(c, slot_count, COLOURS):
                    value = value + jnp.where(held_tall == float(k), start[k, z, rows, :], 0.0)
                packed_a[a, z, mid, :] = value * inside[rows]
        none = jnp.zeros((m, ey), jnp.float32)
        value = jnp.concatenate(
            [none]
            + [tall(jnp.where(slot_rows[r] == span, 1.0, 0.0), BLK // PAD) for r in range(2)]
            + [none],
            axis=0,
        )
        span_tall = tall(span, n_s)
        for k in range(sub_y):
            value = value + jnp.where(span_tall == float(k), start[k, z], 0.0)
        spanning_a[z, mid_s, :] = value * inside * span_map[...]
        return carry

    lax.fori_loop(0, nz, fill, 0)

    receive(0)
    lane_f = lax.broadcasted_iota(jnp.int32, (full, ey), 1)
    border = jnp.logical_or(lane_f < m, lane_f >= ey - m)
    for i in range(n_win):
        block, j = i // per, i % per
        near = jnp.where(lane_f // m == j, strip_in[1, block], strip_in[0, block])
        near = pltpu.roll(near, (-m * j) % ey, axis=1)
        joined[i] = jnp.where(border, near, window[i])
    lane_s = lax.broadcasted_iota(jnp.int32, (ex, ey), 1)
    for z in range(nz):
        here = joined[KX + z, mid_s, :]
        link_xl = harmonic(joined[KX + z, PAD - 1 : PAD - 1 + ex, :], here)
        link_xh = harmonic(here, joined[KX + z, PAD + 1 : PAD + 1 + ex, :])
        here = joined[KY + z, mid_s, :]
        spot = m * (per - 1) + z
        outer = pltpu.roll(strip_in[1, 1, mid_s, :], (-spot) % ey, axis=1)
        link_yl = harmonic(jnp.where(lane_s == 0, outer, pltpu.roll(here, 1, axis=1)), here)
        spot = m * (per - 2) + z
        outer = pltpu.roll(strip_in[0, 1, mid_s, :], (ey - 1 - spot) % ey, axis=1)
        link_yh = harmonic(here, jnp.where(lane_s == ey - 1, outer, pltpu.roll(here, ey - 1, axis=1)))
        links = [link_xl, link_xh, link_yl, link_yh]
        places = [0, 1, 2, 3]
        if z > 0:
            links.append(joined[TZ + z - 1, mid_s, :])
            places.append(4)
        if z < nz - 1:
            links.append(joined[TZ + z, mid_s, :])
            places.append(5)
        total = links[0]
        for link in links[1:]:
            total = total + link
        diagonal = jnp.maximum(total + 0.05 * joined[ST + z, mid_s, :], 0.01)
        factor = (WEIGHT / (1.0 - WEIGHT)) / diagonal
        for place_no, link in zip(places, links):
            value = link * factor
            if place_no == 2:
                value = jnp.where(lane_s > 0, value, 0.0)
            if place_no == 3:
                value = jnp.where(lane_s < ey - 1, value, 0.0)
            coef[place_no, z] = value
            if place_no in (2, 3):
                for a in range(2 * COLOURS):
                    first_row = (a // COLOURS) * BLK
                    coef_y[a, place_no - 2, z] = value[first_row : first_row + rows_p] * tall(
                        same[a, place_no - 2], n_p
                    )

    chunk = rows_p // 2

    def sweep(src, dst, src_s, dst_s):
        def chunk_step(t, carry):
            top = pl.multiple_of(t * chunk, PAD)
            rows_c = pl.ds(top, chunk)
            rows_m = pl.ds(top + PAD, chunk)
            for r in range(2):
                rows = pl.ds(top + r * BLK, chunk)
                for z in range(nz):
                    xl, xh = coef[0, z, rows, :], coef[1, z, rows, :]
                    for c in range(COLOURS):
                        a = r * COLOURS + c
                        cur = src[a, z, rows_m, :]
                        new = cur + xl * src[a, z, pl.ds(top + PAD - 1, chunk), :]
                        new = new + xh * src[a, z, pl.ds(top + PAD + 1, chunk), :]
                        if z > 0:
                            new = new + coef[4, z, rows, :] * src[a, z - 1, rows_m, :]
                        if z < nz - 1:
                            new = new + coef[5, z, rows, :] * src[a, z + 1, rows_m, :]
                        new = new + coef_y[a, 0, z, rows_c, :] * pltpu.roll(cur, 1, axis=1)
                        new = new + coef_y[a, 1, z, rows_c, :] * pltpu.roll(cur, ey - 1, axis=1)
                        dst[a, z, rows_m, :] = new
            return carry

        lax.fori_loop(0, 2, chunk_step, 0)
        for z in range(nz):
            cur = src_s[z, mid_s, :]
            new = cur + coef[0, z] * src_s[z, PAD - 1 : PAD - 1 + ex, :]
            new = new + coef[1, z] * src_s[z, PAD + 1 : PAD + 1 + ex, :]
            if z > 0:
                new = new + coef[4, z] * src_s[z - 1, mid_s, :]
            if z < nz - 1:
                new = new + coef[5, z] * src_s[z + 1, mid_s, :]
            new = new + coef[2, z] * pltpu.roll(cur, 1, axis=1)
            new = new + coef[3, z] * pltpu.roll(cur, ey - 1, axis=1)
            dst_s[z, mid_s, :] = new * span_map[...]

    unscale = (1.0 - WEIGHT) ** SWEEPS
    width = 2 * m
    for turn in range(ITERS):
        here, there = (packed_a, spanning_a), (packed_b, spanning_b)
        for _ in range(SWEEPS):
            sweep(here[0], there[0], here[1], there[1])
            here, there = there, here
        packed, spanning = here
        strips = [jnp.zeros((ex, ey), jnp.float32) for _ in range(2)]
        for z in range(nz):
            sums = []
            for r in range(2):
                value = packed[r * COLOURS, z, mid, :]
                for c in range(1, COLOURS):
                    value = value + packed[r * COLOURS + c, z, mid, :]
                sums.append(value)
            gap = jnp.zeros((ex - rows_p, ey), jnp.float32)
            value = (
                spanning[z, mid_s, :]
                + jnp.concatenate([sums[0], gap], axis=0)
                + jnp.concatenate([gap, sums[1]], axis=0)
            )
            value = value * unscale
            part[turn, z] = value
            for side in range(2):
                first_lane = 0 if side == 0 else ey - width
                spot = (z - (1 - side)) % nz
                moved = pltpu.roll(value, (width * spot - first_lane) % ey, axis=1)
                strips[side] = jnp.where(lane_s // width == spot, moved, strips[side])
        for side in range(2):
            part_strip[turn, side] = strips[side]
        send(turn + 1)
        receive(turn + 1)
        from_right = part_y[turn, 0] + part_d[turn, 0]
        from_left = part_y[turn, 1] + part_d[turn, 1]
        for z in range(nz):
            near = jnp.where(lane_s // width == z, from_left, from_right)
            near = pltpu.roll(near, (-width * z) % ey, axis=1)
            total = part[turn, z] + part_x[turn, z]
            total = total + jnp.where(jnp.logical_or(lane_s < width, lane_s >= ey - width), near, 0.0)
            scale = unscale / jnp.maximum(total, 0.01)
            for r in range(2):
                rows = slice(r * BLK, r * BLK + rows_p)
                for c in range(COLOURS):
                    a = r * COLOURS + c
                    packed_a[a, z, mid, :] = packed[a, z, mid, :] * scale[rows]
            spanning_a[z, mid_s, :] = spanning[z, mid_s, :] * scale

    for phase in range(ITERS + 1):
        sent(phase)


def unpack(packed, spanning, held, span_ref, out_hbm, out, out_sem):
    nb, nz, ex, ey = out.shape
    rows_p = packed.shape[2] - 2 * PAD
    n_p, n_s = rows_p // PAD, ex // PAD
    mid, mid_s = slice(PAD, PAD + rows_p), slice(PAD, PAD + ex)
    gap = jnp.zeros((ex - rows_p, ey), jnp.float32)
    in_top = nb // 2

    def layer(z, carry):
        span_tall = tall(span_ref[...], n_s)
        whole = spanning[z, mid_s, :]
        for k in range(nb):
            c = k % COLOURS
            a = COLOURS + c
            value = jnp.where(tall(held[a], n_p) == float(k), packed[a, z, mid, :], 0.0)
            value = jnp.concatenate([gap, value], axis=0)
            if k < in_top:
                top = jnp.where(tall(held[c], n_p) == float(k), packed[c, z, mid, :], 0.0)
                value = value + jnp.concatenate([top, gap], axis=0)
                value = value + jnp.where(span_tall == float(k), whole, 0.0)
            out[k, z] = value
        pltpu.make_async_copy(out.at[:, z], out_hbm.at[:, z], out_sem.at[z]).start()
        return carry

    lax.fori_loop(0, nz, layer, 0)
    for z in range(nz):
        pltpu.make_async_copy(out.at[:, z], out_hbm.at[:, z], out_sem.at[z]).wait()


def solution(mesh):
    n_gx, n_gy = mesh.shape["gx"], mesh.shape["gy"]

    def body(rock_props, block_slot, bases_start):
        nb, nz, ex, ey = bases_start.shape
        n_win = 4 * nz - 1
        full = ex + 2 * PAD
        rows_p = BLK + 2 * MARGIN
        f32 = jnp.float32
        tx = block_slot.shape[0]
        vmem = pl.BlockSpec(memory_space=pltpu.VMEM)
        anywhere = pl.BlockSpec(memory_space=pl.ANY)
        packed_shape = (2 * COLOURS, nz, rows_p + 2 * PAD, ey)
        held = pl.pallas_call(
            functools.partial(kernel, n_gx, n_gy),
            out_shape=(
                jax.ShapeDtypeStruct(packed_shape, f32),
                jax.ShapeDtypeStruct((nz, full, ey), f32),
                jax.ShapeDtypeStruct((2 * COLOURS, PAD, ey), f32),
                jax.ShapeDtypeStruct((PAD, ey), f32),
            ),
            in_specs=[anywhere, vmem, anywhere],
            out_specs=(vmem,) * 4,
            scratch_shapes=[
                pltpu.VMEM(rock_props.shape, f32),
                pltpu.VMEM(bases_start.shape, f32),
                pltpu.VMEM((n_win, full, ey), f32),
                pltpu.VMEM((n_win, full, ey), f32),
                pltpu.VMEM((2, 2, tx, ey), f32),
                pltpu.VMEM((2, 2, full, ey), f32),
                pltpu.VMEM((6, nz, ex, ey), f32),
                pltpu.VMEM((2 * COLOURS, 2, nz, rows_p, ey), f32),
                pltpu.VMEM((2 * COLOURS, 2, PAD, ey), f32),
                pltpu.VMEM((ex, ey), f32),
                pltpu.VMEM(packed_shape, f32),
                pltpu.VMEM((nz, full, ey), f32),
                pltpu.VMEM((ITERS, nz, ex, ey), f32),
                pltpu.VMEM((ITERS, 2, ex, ey), f32),
                pltpu.VMEM((ITERS, nz, ex, ey), f32),
                pltpu.VMEM((ITERS, 2, ex, ey), f32),
                pltpu.VMEM((ITERS, 2, ex, ey), f32),
                pltpu.SemaphoreType.DMA,
                pltpu.SemaphoreType.DMA,
                pltpu.SemaphoreType.DMA((ITERS + 1, 2 * len(DIRS))),
                pltpu.SemaphoreType.DMA((ITERS + 1, 2 * len(DIRS))),
            ],
            compiler_params=pltpu.CompilerParams(collective_id=0, has_side_effects=True),
        )(rock_props, block_slot, bases_start)
        return pl.pallas_call(
            unpack,
            out_shape=jax.ShapeDtypeStruct(bases_start.shape, f32),
            in_specs=[vmem] * 4,
            out_specs=anywhere,
            scratch_shapes=[pltpu.VMEM(bases_start.shape, f32), pltpu.SemaphoreType.DMA((nz,))],
        )(*held)

    placed = (P(None, None, "gx", "gy"), P("gx", "gy"), P(None, None, "gx", "gy"))
    return jax.shard_map(
        body, mesh=mesh, in_specs=placed, out_specs=P(None, None, "gx", "gy"), check_vma=False
    )
```

```python
import functools

import jax
import jax.numpy as jnp
from jax import lax
from jax.experimental import pallas as pl
from jax.experimental.pallas import tpu as pltpu
from jax.sharding import PartitionSpec as P

MARGIN = 16
BLK = 16
ITERS = 2
SWEEPS = 3
PAD = 8
LANES = 128
COLOURS = 3
WEIGHT = 2.0 / 3.0
MESH = pl.DeviceIdType.MESH
DIRS = ((-1, -1), (1, -1), (-1, 1), (1, 1), (0, -1), (0, 1), (-1, 0), (1, 0))


def harmonic(first_k, second_k):
    return 2.0 * first_k * second_k / jnp.maximum(first_k + second_k, 0.1)


def tall(value, count):
    return jnp.concatenate([value] * count, axis=0)


def kernel(
    n_gx, n_gy,
    rock_hbm, slot_ref, start_hbm, packed_a, spanning_a, held_out, span_out,
    rock, start, window, joined, strip_out, strip_in, coef, coef_y, same, span_map, packed_b, spanning_b,
    part, part_strip, part_x, part_y, part_d,
    rock_sem, start_sem, send_sem, recv_sem,
):
    m = MARGIN
    nb, nz, ex, ey = start.shape
    tx, ty = rock.shape[2], rock.shape[3]
    rows_p = BLK + 2 * m
    full = ex + 2 * PAD
    n_win = window.shape[0]
    KX, KY, ST, TZ = 0, nz, 2 * nz, 3 * nz
    sub_y = ty // BLK
    half = ex // 2

    gx = lax.axis_index("gx")
    gy = lax.axis_index("gy")

    def exists(dx, dy):
        ok = None
        for cond in (
            [gx > 0] if dx < 0 else [gx < n_gx - 1] if dx > 0 else []
        ) + ([gy > 0] if dy < 0 else [gy < n_gy - 1] if dy > 0 else []):
            ok = cond if ok is None else jnp.logical_and(ok, cond)
        return ok

    rock_copy = pltpu.make_async_copy(rock_hbm, rock, rock_sem)
    start_copy = pltpu.make_async_copy(start_hbm, start, start_sem)
    rock_copy.start()
    start_copy.start()

    for i in range(n_win):
        window[i, : PAD + m, :] = jnp.zeros((PAD + m, ey), jnp.float32)
        window[i, PAD + m + tx :, :] = jnp.zeros((PAD + m, ey), jnp.float32)
    strip_in[...] = jnp.zeros_like(strip_in)
    part_x[...] = jnp.zeros_like(part_x)
    part_y[...] = jnp.zeros_like(part_y)
    part_d[...] = jnp.zeros_like(part_d)

    barrier = pltpu.get_barrier_semaphore()
    expected = jnp.int32(0)
    for dx, dy in DIRS:
        there = exists(dx, dy)
        expected = expected + there.astype(jnp.int32)

        @pl.when(there)
        def _(dx=dx, dy=dy):
            pl.semaphore_signal(
                barrier, inc=1, device_id=(gx + dx, gy + dy), device_id_type=MESH
            )

    def rock_messages(dx, dy):
        if dy == 0:
            if dx < 0:
                return [
                    (window.at[0:nz, pl.ds(PAD + m, m + PAD)], window.at[0:nz, pl.ds(PAD + m + tx, m + PAD)]),
                    (window.at[nz:n_win, pl.ds(PAD + m, m)], window.at[nz:n_win, pl.ds(PAD + m + tx, m)]),
                ]
            return [
                (window.at[0:nz, pl.ds(tx, m + PAD)], window.at[0:nz, pl.ds(0, m + PAD)]),
                (window.at[nz:n_win, pl.ds(PAD + tx, m)], window.at[nz:n_win, pl.ds(PAD, m)]),
            ]
        side = 0 if dy < 0 else 1
        if dx == 0:
            return [(strip_out.at[side], strip_in.at[side, :, pl.ds(PAD + m, tx)])]
        if dx < 0:
            return [(strip_out.at[side, :, pl.ds(0, m + PAD)], strip_in.at[side, :, pl.ds(PAD + m + tx, m + PAD)])]
        return [(strip_out.at[side, :, pl.ds(tx - m - PAD, m + PAD)], strip_in.at[side, :, pl.ds(0, m + PAD)])]

    def sum_messages(turn, dx, dy):
        if dy == 0:
            if dx < 0:
                return [(part.at[turn, z, pl.ds(0, half)], part_x.at[turn, z, pl.ds(half, half)]) for z in range(nz)]
            return [(part.at[turn, z, pl.ds(half, half)], part_x.at[turn, z, pl.ds(0, half)]) for z in range(nz)]
        side = 0 if dy < 0 else 1
        if dx == 0:
            return [(part_strip.at[turn, side], part_y.at[turn, side])]
        if dx < 0:
            return [(part_strip.at[turn, side, pl.ds(0, half)], part_d.at[turn, side, pl.ds(half, half)])]
        return [(part_strip.at[turn, side, pl.ds(half, half)], part_d.at[turn, side, pl.ds(0, half)])]

    def copies(phase, dx, dy, layer=None):
        messages = rock_messages(dx, dy) if phase == 0 else sum_messages(phase - 1, dx, dy)
        base = max(2, nz) * DIRS.index((dx, dy))
        return [
            pltpu.make_async_remote_copy(
                src_ref=src,
                dst_ref=dst,
                send_sem=send_sem.at[phase, base + i],
                recv_sem=recv_sem.at[phase, base + i],
                device_id=(gx + dx, gy + dy),
                device_id_type=MESH,
            )
            for i, (src, dst) in enumerate(messages)
            if layer is None or i == layer
        ]

    def send(phase, along_x, layer=None):
        for dx, dy in DIRS:
            if (dy == 0) != along_x:
                continue

            @pl.when(exists(dx, dy))
            def _(dx=dx, dy=dy):
                for copy in copies(phase, dx, dy, layer):
                    copy.start()

    def receive(phase):
        for dx, dy in DIRS:
            @pl.when(exists(-dx, -dy))
            def _(dx=dx, dy=dy):
                for copy in copies(phase, dx, dy):
                    copy.wait_recv()

    def sent(phase):
        for dx, dy in DIRS:
            @pl.when(exists(dx, dy))
            def _(dx=dx, dy=dy):
                for copy in copies(phase, dx, dy):
                    copy.wait_send()

    rock_copy.wait()
    lane_t = lax.broadcasted_iota(jnp.int32, (tx, ey), 1)
    own_rows = slice(PAD + m, PAD + m + tx)

    def place(i, value):
        wide = jnp.concatenate([value, jnp.zeros((tx, ey - ty), jnp.float32)], axis=1)
        window[i, own_rows, :] = pltpu.roll(wide, m, axis=1)

    for z in range(nz):
        place(KX + z, rock[0, z])
        place(KY + z, rock[1, z])
        place(ST + z, rock[3, z])
        if z < nz - 1:
            place(TZ + z, harmonic(rock[2, z], rock[2, z + 1]))
    pl.semaphore_wait(barrier, expected)
    send(0, True)
    per = LANES // m
    for side in range(2):
        first = m if side == 0 else m + ty - m
        extra = 2 * m if side == 0 else m + ty - m - 1
        for block in range(2):
            packed_strip = jnp.zeros((tx, ey), jnp.float32)
            for i in range(block * per, min(n_win, block * per + per)):
                j = (i - block * per - (1 - side)) % per
                moved = pltpu.roll(window[i, own_rows, :], (m * j - first) % ey, axis=1)
                packed_strip = jnp.where(lane_t // m == j, moved, packed_strip)
            if block == 1:
                for z in range(nz):
                    spot = m * (per - 2 + side) + z
                    moved = pltpu.roll(window[KY + z, own_rows, :], (spot - extra) % ey, axis=1)
                    packed_strip = jnp.where(lane_t == spot, moved, packed_strip)
            strip_out[side, block] = packed_strip

    send(0, False)

    lane = lax.broadcasted_iota(jnp.int32, (PAD, ey), 1)
    slot_rows = []
    for r in range(2):
        raw = slot_ref[r * BLK : r * BLK + PAD, :].astype(jnp.float32)
        wide = jnp.concatenate([raw, jnp.full((PAD, ey - ty), -9.0, jnp.float32)], axis=1)
        slot_rows.append(pltpu.roll(wide, m, axis=1))
    in_tile = jnp.logical_and(lane >= m, lane < m + ty)
    last = jnp.max(slot_rows[0], axis=1, keepdims=True)
    first = jnp.min(jnp.where(in_tile, slot_rows[1], 99.0), axis=1, keepdims=True)
    span = jnp.broadcast_to(jnp.where(last == first, last, -5.0), (PAD, ey))
    reach = []
    for r in range(2):
        near = (slot_rows[r], pltpu.roll(slot_rows[r], m, axis=1), pltpu.roll(slot_rows[r], ey - m, axis=1))
        touched = jnp.zeros((PAD, ey), jnp.float32)
        for value in near:
            touched = jnp.where(value == span, 1.0, touched)
        reach.append(touched)
        for c in range(COLOURS):
            held = jnp.full((PAD, ey), -1.0, jnp.float32)
            for value in near:
                colour = value - COLOURS * jnp.floor((value + 0.5) / COLOURS)
                fits = jnp.logical_and(value >= 0.0, jnp.logical_and(colour == float(c), value != span))
                held = jnp.where(fits, value, held)
            a = r * COLOURS + c
            held_out[a] = held
            taken = held >= 0.0
            low = jnp.logical_and(taken, jnp.logical_and(lane > 0, pltpu.roll(held, 1, axis=1) == held))
            high = jnp.logical_and(taken, jnp.logical_and(lane < ey - 1, pltpu.roll(held, ey - 1, axis=1) == held))
            same[a, 0] = jnp.where(low, 1.0, 0.0)
            same[a, 1] = jnp.where(high, 1.0, 0.0)
    span_out[...] = span
    both = jnp.maximum(reach[0], reach[1])
    span_map[...] = jnp.concatenate(
        [tall(reach[0], BLK // PAD), tall(both, (ex - 2 * BLK) // PAD), tall(reach[1], BLK // PAD)], axis=0
    )

    row = lax.broadcasted_iota(jnp.int32, (ex, ey), 0)
    col = lax.broadcasted_iota(jnp.int32, (ex, ey), 1)
    inside = jnp.ones((ex, ey), jnp.float32)
    edge = lambda cond: jnp.where(cond, 0.0, 1.0).astype(jnp.float32)
    inside = inside * jnp.where(row < m, edge(gx == 0), 1.0)
    inside = inside * jnp.where(row >= m + tx, edge(gx == n_gx - 1), 1.0)
    inside = inside * jnp.where(col < m, edge(gy == 0), 1.0)
    inside = inside * jnp.where(col >= m + ty, edge(gy == n_gy - 1), 1.0)

    for ref in (packed_a, packed_b):
        ref[:, :, :PAD, :] = jnp.zeros(ref.shape[:2] + (PAD, ey), jnp.float32)
        ref[:, :, PAD + rows_p :, :] = jnp.zeros(ref.shape[:2] + (PAD, ey), jnp.float32)
    for ref in (spanning_a, spanning_b):
        ref[:, :PAD, :] = jnp.zeros((nz, PAD, ey), jnp.float32)
        ref[:, PAD + ex :, :] = jnp.zeros((nz, PAD, ey), jnp.float32)
    mid = slice(PAD, PAD + rows_p)
    mid_s = slice(PAD, PAD + ex)
    n_p = rows_p // PAD
    n_s = ex // PAD
    start_copy.wait()

    def fill(z, carry):
        for r in range(2):
            rows = slice(r * BLK, r * BLK + rows_p)
            slot_count = sub_y if r == 0 else nb
            for c in range(COLOURS):
                a = r * COLOURS + c
                held = held_out[a]
                own = jnp.where(held == slot_rows[r], 1.0, 0.0)
                none = jnp.zeros((m, ey), jnp.float32)
                value = jnp.concatenate([none, tall(own, BLK // PAD), none], axis=0)
                held_tall = tall(held, n_p)
                for k in range(c, slot_count, COLOURS):
                    value = value + jnp.where(held_tall == float(k), start[k, z, rows, :], 0.0)
                packed_a[a, z, mid, :] = value * inside[rows]
        none = jnp.zeros((m, ey), jnp.float32)
        value = jnp.concatenate(
            [none]
            + [tall(jnp.where(slot_rows[r] == span, 1.0, 0.0), BLK // PAD) for r in range(2)]
            + [none],
            axis=0,
        )
        span_tall = tall(span, n_s)
        for k in range(sub_y):
            value = value + jnp.where(span_tall == float(k), start[k, z], 0.0)
        spanning_a[z, mid_s, :] = value * inside * span_map[...]
        return carry

    lax.fori_loop(0, nz, fill, 0)

    receive(0)
    lane_f = lax.broadcasted_iota(jnp.int32, (full, ey), 1)
    border = jnp.logical_or(lane_f < m, lane_f >= ey - m)
    for i in range(n_win):
        block, j = i // per, i % per
        near = jnp.where(lane_f // m == j, strip_in[1, block], strip_in[0, block])
        near = pltpu.roll(near, (-m * j) % ey, axis=1)
        joined[i] = jnp.where(border, near, window[i])
    lane_s = lax.broadcasted_iota(jnp.int32, (ex, ey), 1)
    for z in range(nz):
        here = joined[KX + z, mid_s, :]
        link_xl = harmonic(joined[KX + z, PAD - 1 : PAD - 1 + ex, :], here)
        link_xh = harmonic(here, joined[KX + z, PAD + 1 : PAD + 1 + ex, :])
        here = joined[KY + z, mid_s, :]
        spot = m * (per - 1) + z
        outer = pltpu.roll(strip_in[1, 1, mid_s, :], (-spot) % ey, axis=1)
        link_yl = harmonic(jnp.where(lane_s == 0, outer, pltpu.roll(here, 1, axis=1)), here)
        spot = m * (per - 2) + z
        outer = pltpu.roll(strip_in[0, 1, mid_s, :], (ey - 1 - spot) % ey, axis=1)
        link_yh = harmonic(here, jnp.where(lane_s == ey - 1, outer, pltpu.roll(here, ey - 1, axis=1)))
        links = [link_xl, link_xh, link_yl, link_yh]
        places = [0, 1, 2, 3]
        if z > 0:
            links.append(joined[TZ + z - 1, mid_s, :])
            places.append(4)
        if z < nz - 1:
            links.append(joined[TZ + z, mid_s, :])
            places.append(5)
        total = links[0]
        for link in links[1:]:
            total = total + link
        diagonal = jnp.maximum(total + 0.05 * joined[ST + z, mid_s, :], 0.01)
        factor = (WEIGHT / (1.0 - WEIGHT)) / diagonal
        for place_no, link in zip(places, links):
            value = link * factor
            if place_no == 2:
                value = jnp.where(lane_s > 0, value, 0.0)
            if place_no == 3:
                value = jnp.where(lane_s < ey - 1, value, 0.0)
            coef[place_no, z] = value
            if place_no in (2, 3):
                for a in range(2 * COLOURS):
                    first_row = (a // COLOURS) * BLK
                    coef_y[a, place_no - 2, z] = value[first_row : first_row + rows_p] * tall(
                        same[a, place_no - 2], n_p
                    )

    chunk = rows_p // 2

    def sweep(src, dst, src_s, dst_s):
        def chunk_step(t, carry):
            top = pl.multiple_of(t * chunk, PAD)
            rows_c = pl.ds(top, chunk)
            rows_m = pl.ds(top + PAD, chunk)
            for r in range(2):
                rows = pl.ds(top + r * BLK, chunk)
                for z in range(nz):
                    xl, xh = coef[0, z, rows, :], coef[1, z, rows, :]
                    for c in range(COLOURS):
                        a = r * COLOURS + c
                        cur = src[a, z, rows_m, :]
                        new = cur + xl * src[a, z, pl.ds(top + PAD - 1, chunk), :]
                        new = new + xh * src[a, z, pl.ds(top + PAD + 1, chunk), :]
                        if z > 0:
                            new = new + coef[4, z, rows, :] * src[a, z - 1, rows_m, :]
                        if z < nz - 1:
                            new = new + coef[5, z, rows, :] * src[a, z + 1, rows_m, :]
                        new = new + coef_y[a, 0, z, rows_c, :] * pltpu.roll(cur, 1, axis=1)
                        new = new + coef_y[a, 1, z, rows_c, :] * pltpu.roll(cur, ey - 1, axis=1)
                        dst[a, z, rows_m, :] = new
            return carry

        lax.fori_loop(0, 2, chunk_step, 0)
        for z in range(nz):
            cur = src_s[z, mid_s, :]
            new = cur + coef[0, z] * src_s[z, PAD - 1 : PAD - 1 + ex, :]
            new = new + coef[1, z] * src_s[z, PAD + 1 : PAD + 1 + ex, :]
            if z > 0:
                new = new + coef[4, z] * src_s[z - 1, mid_s, :]
            if z < nz - 1:
                new = new + coef[5, z] * src_s[z + 1, mid_s, :]
            new = new + coef[2, z] * pltpu.roll(cur, 1, axis=1)
            new = new + coef[3, z] * pltpu.roll(cur, ey - 1, axis=1)
            dst_s[z, mid_s, :] = new * span_map[...]

    unscale = (1.0 - WEIGHT) ** SWEEPS
    width = 2 * m
    for turn in range(ITERS):
        here, there = (packed_a, spanning_a), (packed_b, spanning_b)
        for _ in range(SWEEPS):
            sweep(here[0], there[0], here[1], there[1])
            here, there = there, here
        packed, spanning = here
        strips = [jnp.zeros((ex, ey), jnp.float32) for _ in range(2)]
        for z in range(nz):
            sums = []
            for r in range(2):
                value = packed[r * COLOURS, z, mid, :]
                for c in range(1, COLOURS):
                    value = value + packed[r * COLOURS + c, z, mid, :]
                sums.append(value)
            gap = jnp.zeros((ex - rows_p, ey), jnp.float32)
            value = (
                spanning[z, mid_s, :]
                + jnp.concatenate([sums[0], gap], axis=0)
                + jnp.concatenate([gap, sums[1]], axis=0)
            )
            value = value * unscale
            part[turn, z] = value
            send(turn + 1, True, z)
            for side in range(2):
                first_lane = 0 if side == 0 else ey - width
                spot = (z - (1 - side)) % nz
                moved = pltpu.roll(value, (width * spot - first_lane) % ey, axis=1)
                strips[side] = jnp.where(lane_s // width == spot, moved, strips[side])
        for side in range(2):
            part_strip[turn, side] = strips[side]
        send(turn + 1, False)
        receive(turn + 1)
        from_right = part_y[turn, 0] + part_d[turn, 0]
        from_left = part_y[turn, 1] + part_d[turn, 1]
        for z in range(nz):
            near = jnp.where(lane_s // width == z, from_left, from_right)
            near = pltpu.roll(near, (-width * z) % ey, axis=1)
            total = part[turn, z] + part_x[turn, z]
            total = total + jnp.where(jnp.logical_or(lane_s < width, lane_s >= ey - width), near, 0.0)
            scale = unscale / jnp.maximum(total, 0.01)
            for r in range(2):
                rows = slice(r * BLK, r * BLK + rows_p)
                for c in range(COLOURS):
                    a = r * COLOURS + c
                    packed_a[a, z, mid, :] = packed[a, z, mid, :] * scale[rows]
            spanning_a[z, mid_s, :] = spanning[z, mid_s, :] * scale

    for phase in range(ITERS + 1):
        sent(phase)


def unpack(packed, spanning, held, span_ref, out_hbm, out, out_sem):
    nb, nz, ex, ey = out.shape
    rows_p = packed.shape[2] - 2 * PAD
    n_p, n_s = rows_p // PAD, ex // PAD
    mid, mid_s = slice(PAD, PAD + rows_p), slice(PAD, PAD + ex)
    gap = jnp.zeros((ex - rows_p, ey), jnp.float32)
    in_top = nb // 2

    def layer(z, carry):
        span_tall = tall(span_ref[...], n_s)
        whole = spanning[z, mid_s, :]
        for k in range(nb):
            c = k % COLOURS
            a = COLOURS + c
            value = jnp.where(tall(held[a], n_p) == float(k), packed[a, z, mid, :], 0.0)
            value = jnp.concatenate([gap, value], axis=0)
            if k < in_top:
                top = jnp.where(tall(held[c], n_p) == float(k), packed[c, z, mid, :], 0.0)
                value = value + jnp.concatenate([top, gap], axis=0)
                value = value + jnp.where(span_tall == float(k), whole, 0.0)
            out[k, z] = value
        pltpu.make_async_copy(out.at[:, z], out_hbm.at[:, z], out_sem.at[z]).start()
        return carry

    lax.fori_loop(0, nz, layer, 0)
    for z in range(nz):
        pltpu.make_async_copy(out.at[:, z], out_hbm.at[:, z], out_sem.at[z]).wait()


def solution(mesh):
    n_gx, n_gy = mesh.shape["gx"], mesh.shape["gy"]

    def body(rock_props, block_slot, bases_start):
        nb, nz, ex, ey = bases_start.shape
        n_win = 4 * nz - 1
        full = ex + 2 * PAD
        rows_p = BLK + 2 * MARGIN
        f32 = jnp.float32
        tx = block_slot.shape[0]
        vmem = pl.BlockSpec(memory_space=pltpu.VMEM)
        anywhere = pl.BlockSpec(memory_space=pl.ANY)
        packed_shape = (2 * COLOURS, nz, rows_p + 2 * PAD, ey)
        held = pl.pallas_call(
            functools.partial(kernel, n_gx, n_gy),
            out_shape=(
                pltpu.VMEM(packed_shape, f32),
                pltpu.VMEM((nz, full, ey), f32),
                pltpu.VMEM((2 * COLOURS, PAD, ey), f32),
                pltpu.VMEM((PAD, ey), f32),
            ),
            in_specs=[anywhere, vmem, anywhere],
            out_specs=(vmem,) * 4,
            scratch_shapes=[
                pltpu.VMEM(rock_props.shape, f32),
                pltpu.VMEM(bases_start.shape, f32),
                pltpu.VMEM((n_win, full, ey), f32),
                pltpu.VMEM((n_win, full, ey), f32),
                pltpu.VMEM((2, 2, tx, ey), f32),
                pltpu.VMEM((2, 2, full, ey), f32),
                pltpu.VMEM((6, nz, ex, ey), f32),
                pltpu.VMEM((2 * COLOURS, 2, nz, rows_p, ey), f32),
                pltpu.VMEM((2 * COLOURS, 2, PAD, ey), f32),
                pltpu.VMEM((ex, ey), f32),
                pltpu.VMEM(packed_shape, f32),
                pltpu.VMEM((nz, full, ey), f32),
                pltpu.VMEM((ITERS, nz, ex, ey), f32),
                pltpu.VMEM((ITERS, 2, ex, ey), f32),
                pltpu.VMEM((ITERS, nz, ex, ey), f32),
                pltpu.VMEM((ITERS, 2, ex, ey), f32),
                pltpu.VMEM((ITERS, 2, ex, ey), f32),
                pltpu.SemaphoreType.DMA,
                pltpu.SemaphoreType.DMA,
                pltpu.SemaphoreType.DMA((ITERS + 1, max(2, nz) * len(DIRS))),
                pltpu.SemaphoreType.DMA((ITERS + 1, max(2, nz) * len(DIRS))),
            ],
            compiler_params=pltpu.CompilerParams(collective_id=0, has_side_effects=True),
        )(rock_props, block_slot, bases_start)
        return pl.pallas_call(
            unpack,
            out_shape=jax.ShapeDtypeStruct(bases_start.shape, f32),
            in_specs=[vmem] * 4,
            out_specs=anywhere,
            scratch_shapes=[pltpu.VMEM(bases_start.shape, f32), pltpu.SemaphoreType.DMA((nz,))],
        )(*(pltpu.with_memory_space_constraint(value, pltpu.VMEM) for value in held))

    placed = (P(None, None, "gx", "gy"), P("gx", "gy"), P(None, None, "gx", "gy"))
    return jax.shard_map(
        body, mesh=mesh, in_specs=placed, out_specs=P(None, None, "gx", "gy"), check_vma=False
    )
```
